256 devices in a mesh: seq: 64 (over y_hi, x, z), tensor: 4 (over y_lo, core).
Axes of the slice: x: 4, y: 4 (y_hi: 2, y_lo: 2; y = y_hi * 2 + y_lo), z: 8, core: 2. Of those that a mesh axis runs over, the one named last changes fastest.
Arguments:
- latents: bfloat16 [8192, 2560], P('seq'), may hold values from -6 to 6
- levels: int32 [64], P('seq'), may hold values from 0 to 999
- head_slot: int32 [1], replicated, may hold values from 0 to 63
- fresh_noise: bfloat16 [128, 2560], P(None, 'tensor'), may hold values from -6 to 6
- ada_weight: bfloat16 [256, 3, 2560], P(None, None, 'tensor'), may hold values from -0.375 to 0.375
- qkv_weight: bfloat16 [2560, 3, 1536], P(None, None, 'tensor'), may hold values from -0.125 to 0.125
- q_gain: float32 [128], replicated, may hold values from 0.5 to 2.5
- k_gain: float32 [128], replicated, may hold values from 0.5 to 2.5
- out_weight: bfloat16 [1536, 2560], P('tensor'), may hold values from -0.15625 to 0.15625
Outputs:
- window: bfloat16 [8192, 2560], P('seq', 'tensor')
- clean: bfloat16 [128, 2560], P('seq', 'tensor')
The draws below stay inside these ranges and needn't reach their ends.
All inputs are finite; a program needn't handle non-finite values.
Results may differ from the reference program's by a relative error of at most 0.0053.
Values may be sent and summed in bfloat16 or wider, within the bound.
No kernel may reach another device: no remote copies, remote signals or barrier semaphores. Data moves between devices by JAX's collectives and lax.ppermute only.
A program may use at most 64 MiB of HBM per device.

```python
import math
import jax
import jax.numpy as jnp
from jax import lax

D = 2560
HEADS = 12
HD = 128
TEMB = 256
LEVELS = 1000
GROUP = 128
GROUPS = 64
FRAMES = 8192


def set_ends(drawn, rng, least, high):
    dims = drawn.shape
    place = [jax.random.randint(jax.random.fold_in(rng, axis), (), 0, dims[axis]) for axis in range(len(dims))]
    drawn = drawn.at[tuple(place)].set(least)
    longest = dims.index(max(dims))
    place[longest] = (place[longest] + 1) % dims[longest]
    return drawn.at[tuple(place)].set(high)


def block_levels(key, dims, cuts, least, top_value):
    loudness, own = 1.0, jax.random.fold_in(key, 6)
    for position, shards_of in cuts:
        draws = jnp.exp(jax.random.uniform(jax.random.fold_in(own, position), (shards_of,), jnp.float32, least / len(cuts), top_value / len(cuts)))
        loudness = loudness * jnp.repeat(draws, dims[position] // shards_of).reshape([-1 if axis == position else 1 for axis in range(len(dims))])
    return loudness


def noise(key, shape, scale, limit, cuts=(), held_as=jnp.bfloat16):
    factor_of = block_levels(key, shape, cuts, -0.22, 0.18) if cuts else 1.0
    array = jax.random.normal(key, shape, jnp.float32) * scale * factor_of
    return jnp.minimum(jnp.maximum(array, -limit), limit).astype(held_as)


def setup_inputs(seed: int = 0) -> dict:
    splits = jax.random.split(jax.random.key(seed), 10)
    return {
        "latents": noise(splits[0], (FRAMES, D), 1.0, 6.0, ((0, 64),)),
        "levels": set_ends(jax.random.randint(splits[1], (GROUPS,), 0, LEVELS), jax.random.fold_in(splits[1], 1), 0, LEVELS - 1).astype(jnp.int32),
        "head_slot": jax.random.randint(splits[2], (1,), 0, GROUPS).astype(jnp.int32),
        "fresh_noise": noise(splits[3], (GROUP, D), 1.0, 6.0, ((1, 4),)),
        "ada_weight": noise(splits[4], (TEMB, 3, D), TEMB ** -0.5, 0.375, ((2, 4),)),
        "qkv_weight": noise(splits[5], (D, 3, HEADS * HD), D ** -0.5, 0.125, ((2, 4),)),
        "q_gain": jnp.clip(jnp.exp(jax.random.uniform(splits[6], (HD,), jnp.float32, math.log(0.5), math.log(2.5))), 0.5, 2.5),
        "k_gain": jnp.clip(jnp.exp(jax.random.uniform(splits[7], (HD,), jnp.float32, math.log(0.5), math.log(2.5))), 0.5, 2.5),
        "out_weight": noise(splits[8], (HEADS * HD, D), (HEADS * HD) ** -0.5, 0.15625, ((0, 4),)),
    }


def modulation(levels, ada_weight):
    half_width = TEMB // 2
    frequency = jnp.exp(-math.log(10000.0) * jnp.arange(half_width, dtype=jnp.float32) / half_width)
    angles = levels.astype(jnp.float32)[:, None] * frequency[None, :]
    embedding = jax.nn.silu(jnp.concatenate([jnp.cos(angles), jnp.sin(angles)], axis=1)).astype(jnp.bfloat16)
    flat = jnp.dot(embedding, ada_weight.reshape(TEMB, 3 * D), preferred_element_type=jnp.float32)
    return flat.reshape(-1, 3, D)

def modulate(states, offset_terms, scale_terms):
    average = lax.optimization_barrier(jnp.mean(states, axis=-1, keepdims=True))
    centered = states - average
    variance = lax.optimization_barrier(jnp.mean(centered * centered, axis=-1, keepdims=True))
    normed = centered * lax.rsqrt(variance + 1e-06)
    return (normed * (1.0 + scale_terms) + offset_terms).astype(jnp.bfloat16)

def rms_scaled(matrix, gain_vector, factor):
    power = lax.optimization_barrier(jnp.mean(matrix * matrix, axis=-1, keepdims=True))
    return (matrix * lax.rsqrt(power + 1e-06) * gain_vector * factor).astype(jnp.bfloat16)

def project(hidden, qkv_weight, q_gain, k_gain):
    projected_all = jnp.dot(hidden, qkv_weight.reshape(D, 3 * HEADS * HD), preferred_element_type=jnp.float32)
    projected_all = projected_all.reshape(-1, 3, HEADS, HD)
    queries = rms_scaled(projected_all[:, 0], q_gain, 1.0 / math.sqrt(HD))
    keys = rms_scaled(projected_all[:, 1], k_gain, 1.0)
    values = projected_all[:, 2].astype(jnp.bfloat16)
    return (queries, keys, values)

def reference(latents, levels, head_slot, fresh_noise, ada_weight, qkv_weight, q_gain, k_gain, out_weight):
    oldest = head_slot[0].astype(jnp.int32)
    modulations = modulation(levels, ada_weight)
    states = latents.astype(jnp.float32).reshape(GROUPS, GROUP, D)
    hidden = modulate(states, modulations[:, 0][:, None], modulations[:, 1][:, None]).reshape(GROUPS * GROUP, D)
    queries, keys, values = project(hidden, qkv_weight, q_gain, k_gain)
    query_blocks = queries.reshape(GROUPS, GROUP, HEADS, HD)
    key_blocks = keys.reshape(GROUPS, GROUP, HEADS, HD)
    value_blocks = values.reshape(GROUPS, GROUP, HEADS, HD)
    block_ranks = (jnp.arange(GROUPS, dtype=jnp.int32) - oldest) % GROUPS

    def one_block(query_index):
        query_tile = query_blocks[query_index].astype(jnp.float32)
        initial = (jnp.zeros((HEADS, GROUP), jnp.float32), jnp.zeros((GROUP, HEADS, HD), jnp.float32))

        def absorb(state_now, key_index):

            def update_state(state_old):
                running_sum, weighted = state_old
                key_tile = key_blocks[key_index].astype(jnp.float32)
                value_tile = value_blocks[key_index].astype(jnp.float32)
                scores = jnp.einsum('qhd,khd->hqk', query_tile, key_tile)
                weights = jnp.exp(scores)
                running_sum = running_sum + lax.optimization_barrier(jnp.sum(weights, axis=-1))
                rounded = lax.optimization_barrier(weights.astype(jnp.bfloat16)).astype(jnp.float32)
                weighted = weighted + jnp.einsum('hqk,khd->qhd', rounded, value_tile)
                return (running_sum, weighted)

            def keep_state(state_old):
                return state_old
            visible = block_ranks[key_index] <= block_ranks[query_index]
            return (lax.cond(visible, update_state, keep_state, state_now), None)
        finished, unused = lax.scan(absorb, initial, jnp.arange(GROUPS, dtype=jnp.int32))
        return (finished[1] / finished[0].T[..., None]).astype(jnp.bfloat16)
    attended = lax.map(one_block, jnp.arange(GROUPS, dtype=jnp.int32)).reshape(GROUPS * GROUP, HEADS * HD)
    projected = jnp.dot(attended, out_weight, preferred_element_type=jnp.float32).reshape(GROUPS, GROUP, D)
    updated = (states + modulations[:, 2][:, None] * projected).astype(jnp.bfloat16)
    clean = lax.dynamic_index_in_dim(updated, oldest, 0, keepdims=False)
    leaving = (block_ranks == 0)[:, None, None]
    window = jnp.where(leaving, fresh_noise[None], updated).reshape(GROUPS * GROUP, D)
    return (window, clean)
```

```python
import functools
import math

import jax
import jax.numpy as jnp
from jax import lax
from jax.experimental import pallas as pl
from jax.experimental.pallas import tpu as pltpu
from jax.sharding import Mesh
from jax.sharding import PartitionSpec as P

F32 = jnp.float32
BF16 = jnp.bfloat16
COLS = 8
LINE = 8
BLOCKS = COLS * LINE
ROWS = 128
HD = 128
NH = 3
D = 2560
QW = D // 4
QROWS = NH * ROWS
EXTRA = 144
SEND = QROWS + EXTRA
BACK = QROWS + 16
OUTROWS = ROWS + 16


def vmem(n):
    return [pl.BlockSpec(memory_space=pltpu.VMEM)] * n


def smem():
    return pl.BlockSpec(memory_space=pltpu.SMEM)


def params(mib=48):
    return pltpu.CompilerParams(vmem_limit_bytes=mib << 20)


def dot(a, b):
    return jnp.dot(a, b, preferred_element_type=F32)


def dot_t(a, b):
    return lax.dot_general(a, b, (((1,), (1,)), ((), ())), preferred_element_type=F32)


def modulation_kernel(level_ref, ada_ref, out_ref):
    half = 128
    index = lax.broadcasted_iota(jnp.int32, (16, 2 * half), 1)
    place = jnp.where(index < half, index, index - half).astype(F32)
    frequency = jnp.exp(-math.log(10000.0) * place / half)
    angle = level_ref[0].astype(F32) * frequency
    wave = jnp.where(index < half, jnp.cos(angle), jnp.sin(angle))
    embedding = (wave * (1.0 / (1.0 + jnp.exp(-wave)))).astype(BF16)
    for j in range(3):
        row = dot(embedding, ada_ref[j])[0:1]
        out_ref[pl.ds(j, 1), :] = row


def modulation(levels, ada):
    return pl.pallas_call(
        modulation_kernel,
        out_shape=jax.ShapeDtypeStruct((8, QW), F32),
        in_specs=[smem()] + vmem(1),
        out_specs=vmem(1)[0],
        compiler_params=params(16),
        name="modulation",
    )(levels, ada)


def rms_rounded(matrix, gain, factor):
    power = jnp.mean(matrix * matrix, axis=-1, keepdims=True)
    return (matrix * lax.rsqrt(power + 1e-06) * gain * factor).astype(BF16)


def kv_kernel(lat_ref, mod_ref, w_ref, gain_ref, hidden_ref, kv_ref):
    step = pl.program_id(0)

    @pl.when(step == 0)
    def _():
        states = lat_ref[...].astype(F32)
        average = jnp.mean(states, axis=-1, keepdims=True)
        centered = states - average
        variance = jnp.mean(centered * centered, axis=-1, keepdims=True)
        normed = centered * lax.rsqrt(variance + 1e-06)
        for t in range(4):
            piece = normed[:, t * QW : (t + 1) * QW]
            shift = mod_ref[t, 0:1, :]
            scale = mod_ref[t, 1:2, :]
            hidden_ref[:, t * QW : (t + 1) * QW] = (piece * (1.0 + scale) + shift).astype(BF16)

    out = dot(hidden_ref[...], w_ref[0])

    @pl.when(step == 0)
    def _():
        for h in range(NH):
            kv_ref[h * ROWS : (h + 1) * ROWS, :] = rms_rounded(
                out[:, h * HD : (h + 1) * HD], gain_ref[...], 1.0
            )

    @pl.when(step == 1)
    def _():
        for h in range(NH):
            kv_ref[QROWS + h * ROWS : QROWS + (h + 1) * ROWS, :] = out[
                :, h * HD : (h + 1) * HD
            ].astype(BF16)


def keys_values(latents, mods, w, k_gain):
    full = lambda *shape: pl.BlockSpec(shape, lambda i: (0,) * len(shape))
    return pl.pallas_call(
        kv_kernel,
        grid=(2,),
        out_shape=(
            jax.ShapeDtypeStruct((ROWS, D), BF16),
            jax.ShapeDtypeStruct((2 * QROWS, HD), BF16),
        ),
        in_specs=[
            full(ROWS, D),
            full(4, 8, QW),
            pl.BlockSpec((1, D, QROWS), lambda i: (i + 1, 0, 0)),
            full(1, HD),
        ],
        out_specs=(full(ROWS, D), full(2 * QROWS, HD)),
        compiler_params=params(),
        name="keys_values",
    )(latents, mods, w, k_gain)


def query_kernel(scal_ref, hidden_ref, w_ref, gain_ref, kv_ref, lat_ref, mod_ref, out_ref):
    out = dot(hidden_ref[...], w_ref[0])
    queries = []
    for h in range(NH):
        q = rms_rounded(out[:, h * HD : (h + 1) * HD], gain_ref[...], 1.0 / math.sqrt(HD))
        queries.append(q)
        for c in range(COLS):
            out_ref[c, h * ROWS : (h + 1) * ROWS, :] = q
    for h in range(NH):
        keys = kv_ref[h * ROWS : (h + 1) * ROWS, :]
        values = kv_ref[QROWS + h * ROWS : QROWS + (h + 1) * ROWS, :]
        weights = jnp.exp(dot_t(queries[h], keys))
        total = jnp.sum(weights, axis=-1, keepdims=True)
        attended = (dot(weights.astype(BF16), values) / total).astype(BF16)
        for c in range(COLS):
            out_ref[c, QROWS + h * 16 : QROWS + (h + 1) * 16, :] = attended[c * 16 : (c + 1) * 16]
    first = pl.multiple_of(scal_ref[3] * QW, 128)
    for k in range(5):
        piece = lat_ref[:, pl.ds(first + k * 128, 128)]
        for c in range(COLS):
            at = QROWS + (NH + k) * 16
            out_ref[c, at : at + 16, :] = piece[c * 16 : (c + 1) * 16]
    rows = [mod_ref[2:3, k * 128 : (k + 1) * 128] for k in range(5)]
    high = [row.astype(BF16).astype(F32) for row in rows]
    low = [row - top for row, top in zip(rows, high)]
    gate = jnp.concatenate(high + low + [jnp.zeros((6, 128), F32)], axis=0).astype(BF16)
    for c in range(COLS):
        out_ref[c, QROWS + 128 : SEND, :] = gate


def query_parts(scal, hidden, w, q_gain, kv, latents, mod):
    full = lambda *shape: pl.BlockSpec(shape, lambda i: (0,) * len(shape))
    return pl.pallas_call(
        query_kernel,
        grid=(1,),
        out_shape=jax.ShapeDtypeStruct((COLS, SEND, HD), BF16),
        in_specs=[
            smem(),
            full(ROWS, D),
            pl.BlockSpec((1, D, QROWS), lambda i: (0, 0, 0)),
            full(1, HD),
            full(2 * QROWS, HD),
            full(ROWS, D),
            full(8, QW),
        ],
        out_specs=full(COLS, SEND, HD),
        compiler_params=params(),
        name="queries",
    )(scal, hidden, w, q_gain, kv, latents, mod)


def attention_kernel(scal_ref, q_ref, kv_ref, out_ref):
    column, line, oldest = scal_ref[0], scal_ref[1], scal_ref[2]
    part = 4
    key_block = lax.broadcasted_iota(jnp.int32, (1, LINE * ROWS), 1) // ROWS
    key_rank = (column * LINE + key_block - oldest) & (BLOCKS - 1)
    lane = lax.broadcasted_iota(jnp.int32, (ROWS, 128), 1)
    row16 = lax.broadcasted_iota(jnp.int32, (16, 128), 0)
    for first in range(0, COLS, part):
        query_block = first + lax.broadcasted_iota(jnp.int32, (part * ROWS, 1), 0) // ROWS
        query_rank = (query_block * LINE + line - oldest) & (BLOCKS - 1)
        seen = key_rank <= query_rank
        totals = []
        for h in range(NH):
            q = q_ref[first : first + part, h * ROWS : (h + 1) * ROWS, :].reshape(part * ROWS, HD)
            keys = kv_ref[:, h * ROWS : (h + 1) * ROWS, :].reshape(LINE * ROWS, HD)
            values = kv_ref[:, QROWS + h * ROWS : QROWS + (h + 1) * ROWS, :].reshape(
                LINE * ROWS, HD
            )
            weights = jnp.where(seen, jnp.exp(dot_t(q, keys)), 0.0)
            totals.append(jnp.sum(weights, axis=-1, keepdims=True))
            products = dot(weights.astype(BF16), values).astype(BF16)
            for b in range(part):
                out_ref[first + b, h * ROWS : (h + 1) * ROWS, :] = products[
                    b * ROWS : (b + 1) * ROWS
                ]
        for b in range(part):
            tile = jnp.zeros((ROWS, 128), F32)
            for h in range(NH):
                total = totals[h][b * ROWS : (b + 1) * ROWS]
                tile = jnp.where((lane == h) | (lane == h + NH), total, tile)
            tile = tile.T[0:16]
            high = tile.astype(BF16).astype(F32)
            out_ref[first + b, QROWS:BACK, :] = jnp.where(row16 < NH, high, tile - high).astype(
                BF16
            )


def partial_attention(scal, queries, kv):
    return pl.pallas_call(
        attention_kernel,
        out_shape=jax.ShapeDtypeStruct((COLS, BACK, HD), BF16),
        in_specs=[smem()] + vmem(2),
        out_specs=vmem(1)[0],
        compiler_params=params(),
        name="attention",
    )(scal, queries, kv)


def output_kernel(back_ref, leaving_ref, w_ref, out_ref, held_ref):
    sums = back_ref[0].astype(F32)
    for c in range(1, COLS):
        sums = sums + back_ref[c].astype(F32)
    tile = jnp.concatenate([sums[QROWS:BACK], jnp.zeros((ROWS - 16, 128), F32)], axis=0).T
    for h in range(NH):
        total = tile[:, h : h + 1] + tile[:, h + NH : h + NH + 1]
        held_ref[0:ROWS, h * HD : (h + 1) * HD] = (sums[h * ROWS : (h + 1) * ROWS] / total).astype(
            BF16
        )
        held_ref[ROWS:OUTROWS, h * HD : (h + 1) * HD] = jnp.concatenate(
            [leaving_ref[2 * h : 2 * h + 2, :].astype(F32), jnp.zeros((14, HD), F32)], axis=0
        ).astype(BF16)
    for t in range(4):
        out_ref[t] = dot(held_ref[...], w_ref[:, t * QW : (t + 1) * QW]).astype(BF16)


def output_parts(back, leaving, w):
    return pl.pallas_call(
        output_kernel,
        out_shape=jax.ShapeDtypeStruct((4, OUTROWS, QW), BF16),
        in_specs=vmem(3),
        out_specs=vmem(1)[0],
        scratch_shapes=[pltpu.VMEM((OUTROWS, QROWS), BF16)],
        compiler_params=params(),
        name="output",
    )(back, leaving, w)


def final_kernel(scal_ref, parts_ref, lat_ref, mod_ref, leaving_ref, fresh_ref, window_ref, clean_ref):
    projected = parts_ref[0].astype(F32)
    for t in range(1, 4):
        projected = projected + parts_ref[t].astype(F32)
    first = pl.multiple_of(scal_ref[3] * QW, 128)
    own = scal_ref[0] * LINE + scal_ref[1] == scal_ref[2]
    leaving = leaving_ref[...].astype(F32)
    for k in range(5):
        at = slice(k * 128, (k + 1) * 128)
        states = lat_ref[:, pl.ds(first + k * 128, 128)].astype(F32)
        updated = (states + mod_ref[2:3, at] * projected[0:ROWS, at]).astype(BF16)
        window_ref[:, at] = jnp.where(own, fresh_ref[:, at], updated)
        gate = leaving[16 + k : 17 + k] + leaving[21 + k : 22 + k]
        old = leaving[2 * (NH + k) : 2 * (NH + k) + 2]
        clean_ref[:, at] = (old + gate * projected[ROWS : ROWS + 2, at]).astype(BF16)


def finish(scal, parts, latents, mod, leaving, fresh):
    return pl.pallas_call(
        final_kernel,
        out_shape=(
            jax.ShapeDtypeStruct((ROWS, QW), BF16),
            jax.ShapeDtypeStruct((2, QW), BF16),
        ),
        in_specs=[smem()] + vmem(5),
        out_specs=tuple(vmem(2)),
        compiler_params=params(),
        name="finish",
    )(scal, parts, latents, mod, leaving, fresh)


def local(
    latents, levels, head_slot, fresh_noise, ada_weight, qkv_weight, q_gain, k_gain, out_weight
):
    columns, line, tensor = ("yh", "x"), "z", ("yl", "core")
    oldest = head_slot[0]
    scal = jnp.stack(
        [lax.axis_index(columns), lax.axis_index(line), oldest, lax.axis_index(tensor)]
    ).astype(jnp.int32)
    ada = jnp.transpose(ada_weight, (1, 0, 2))
    w = jnp.transpose(qkv_weight, (1, 0, 2))
    mod = modulation(levels, ada)
    mods = lax.all_gather(mod, tensor, axis=0, tiled=False)
    hidden, kv = keys_values(latents, mods, w, k_gain[None])
    kv_all = lax.all_gather(kv, line, axis=0, tiled=False)
    sent = query_parts(scal, hidden, w, q_gain[None], kv, latents, mod)
    came = lax.all_to_all(sent, columns, 0, 0)
    extra = lax.dynamic_slice(
        came, (oldest // LINE, QROWS, 0), (1, EXTRA, HD)
    )[0]
    rows = extra[:128].reshape(8, LINE, 2, HD).transpose(1, 0, 2, 3).reshape(LINE, 16, HD)
    onward = jnp.concatenate(
        [rows, jnp.broadcast_to(extra[128:][None], (LINE, 16, HD))], axis=1
    )
    arrived = lax.all_to_all(onward, line, 0, 0)
    leaving = lax.dynamic_slice(arrived, (oldest % LINE, 0, 0), (1, 32, HD))[0]
    partial = partial_attention(scal, came, kv_all)
    back = lax.all_to_all(partial, columns, 0, 0)
    parts = output_parts(back, leaving, out_weight)
    parts = lax.all_to_all(parts, tensor, 0, 0)
    return finish(scal, parts, latents, mod, leaving, fresh_noise)


def solution(mesh):
    fine = Mesh(mesh.devices.reshape(2, 4, 8, 2, 2), ("yh", "x", "z", "yl", "core"))
    seq, tensor = ("yh", "x", "z"), ("yl", "core")
    return jax.shard_map(
        local,
        mesh=fine,
        in_specs=(
            P(seq, None),
            P(seq),
            P(),
            P(None, tensor),
            P(None, None, tensor),
            P(None, None, tensor),
            P(),
            P(),
            P(tensor, None),
        ),
        out_specs=(P(seq, tensor), P(seq, tensor)),
        check_vma=False,
    )
```

```python
import functools
import math

import jax
import jax.numpy as jnp
from jax import lax
from jax.experimental import pallas as pl
from jax.experimental.pallas import tpu as pltpu
from jax.sharding import Mesh
from jax.sharding import PartitionSpec as P

F32 = jnp.float32
BF16 = jnp.bfloat16
COLS = 8
LINE = 8
BLOCKS = COLS * LINE
ROWS = 128
HD = 128
NH = 3
D = 2560
QW = D // 4
QROWS = NH * ROWS
KV = 2 * QROWS
EXTRA = 144
SEND = KV + EXTRA
BACK = QROWS + 16
RETURN = BACK + 32
OUTROWS = ROWS + 16
AWAY = (0, -1, 1, -2, 2, -3, 3, 4)
TURNS = ((6, 7), (4, 5), (2, 3), (0, 1))


def vmem(n):
    return [pl.BlockSpec(memory_space=pltpu.VMEM)] * n


def hbm():
    return pl.BlockSpec(memory_space=pltpu.MemorySpace.HBM)


def smem():
    return pl.BlockSpec(memory_space=pltpu.SMEM)


def params(mib=48):
    return pltpu.CompilerParams(vmem_limit_bytes=mib << 20)


def dot(a, b):
    return jnp.dot(a, b, preferred_element_type=F32)


def dot_t(a, b):
    return lax.dot_general(a, b, (((1,), (1,)), ((), ())), preferred_element_type=F32)


def opening_kernel(
    level_ref, scal_ref, ada_ref, lat_ref, qg_ref, kg_ref, mod_ref, normed_ref, own_ref
):
    half = 128
    index = lax.broadcasted_iota(jnp.int32, (16, 2 * half), 1)
    place = jnp.where(index < half, index, index - half).astype(F32)
    frequency = jnp.exp(-math.log(10000.0) * place / half)
    angle = level_ref[0].astype(F32) * frequency
    wave = jnp.where(index < half, jnp.cos(angle), jnp.sin(angle))
    embedding = (wave * (1.0 / (1.0 + jnp.exp(-wave)))).astype(BF16)
    for j in range(3):
        mod_ref[pl.ds(j, 1), :] = dot(embedding, ada_ref[j])[0:1]
    mod_ref[3:4, 0:HD] = qg_ref[...]
    mod_ref[4:5, 0:HD] = kg_ref[...]
    states = lat_ref[...].astype(F32)
    average = jnp.mean(states, axis=-1, keepdims=True)
    centered = states - average
    variance = jnp.mean(centered * centered, axis=-1, keepdims=True)
    normed_ref[...] = centered * lax.rsqrt(variance + 1e-06)
    first = pl.multiple_of(scal_ref[3] * QW, 128)
    for k in range(5):
        own_ref[:, k * 128 : (k + 1) * 128] = lat_ref[:, pl.ds(first + k * 128, 128)]


def opening(levels, scal, ada, latents, q_gain, k_gain):
    return pl.pallas_call(
        opening_kernel,
        out_shape=(
            jax.ShapeDtypeStruct((8, QW), F32),
            jax.ShapeDtypeStruct((ROWS, D), F32),
            jax.ShapeDtypeStruct((ROWS, QW), BF16),
        ),
        in_specs=[smem(), smem()] + vmem(4),
        out_specs=tuple(vmem(3)),
        compiler_params=params(16),
        name="opening",
    )(levels, scal, ada, latents, q_gain, k_gain)


def rms_rounded(matrix, gain, factor):
    power = jnp.mean(matrix * matrix, axis=-1, keepdims=True)
    return (matrix * lax.rsqrt(power + 1e-06) * gain * factor).astype(BF16)


def front_kernel(
    normed_ref, mods_ref, mod_ref, own_ref, w_ref, q_ref, out_ref, hidden_ref, piece_ref, cut_ref
):
    for t in range(4):
        piece = normed_ref[:, t * QW : (t + 1) * QW]
        shift = mods_ref[t, 0:1, :]
        scale = mods_ref[t, 1:2, :]
        hidden_ref[:, t * QW : (t + 1) * QW] = (piece * (1.0 + scale) + shift).astype(BF16)
    for k in range(5):
        piece_ref[NH + k] = own_ref[:, k * 128 : (k + 1) * 128].astype(F32)
    rows = [mod_ref[2:3, k * 128 : (k + 1) * 128] for k in range(5)]
    high = [row.astype(BF16).astype(F32) for row in rows]
    low = [row - top for row, top in zip(rows, high)]
    gate = jnp.concatenate(high + low + [jnp.zeros((6, 128), F32)], axis=0).astype(BF16)
    hidden = hidden_ref[...]
    keys_all = dot(hidden, w_ref[1])
    values_all = dot(hidden, w_ref[2])
    queries_all = dot(hidden, w_ref[0])
    for h in range(NH):
        at = slice(h * HD, (h + 1) * HD)
        keys = rms_rounded(keys_all[:, at], mod_ref[4:5, 0:HD], 1.0)
        values = values_all[:, at].astype(BF16)
        q = rms_rounded(queries_all[:, at], mod_ref[3:4, 0:HD], 1.0 / math.sqrt(HD))
        q_ref[at, :] = q
        for c in range(COLS):
            out_ref[c, h * ROWS : (h + 1) * ROWS, :] = keys
            out_ref[c, QROWS + h * ROWS : QROWS + (h + 1) * ROWS, :] = values
        weights = jnp.exp(dot_t(q, keys))
        total = jnp.sum(weights, axis=-1, keepdims=True)
        attended = (dot(weights.astype(BF16), values) / total).astype(BF16)
        piece_ref[h] = attended.astype(F32)
    for k in range(8):
        for r in range(2):
            cut_ref[pl.ds(2 * k + r, BLOCKS, stride=16), :] = piece_ref[
                k, pl.ds(r, BLOCKS, stride=2), :
            ]
    for c in range(COLS):
        out_ref[c, KV : KV + 128, :] = cut_ref[c * 128 : (c + 1) * 128, :].astype(BF16)
        out_ref[c, KV + 128 : SEND, :] = gate


def front(normed, mods, mod, own, w):
    return pl.pallas_call(
        front_kernel,
        out_shape=(
            jax.ShapeDtypeStruct((QROWS, HD), BF16),
            jax.ShapeDtypeStruct((COLS, SEND, HD), BF16),
        ),
        in_specs=vmem(5),
        out_specs=tuple(vmem(2)),
        scratch_shapes=[
            pltpu.VMEM((ROWS, D), BF16),
            pltpu.VMEM((8, ROWS, 128), F32),
            pltpu.VMEM((BLOCKS * 16, 128), F32),
        ],
        compiler_params=params(16),
        name="front",
    )(normed, mods, mod, own, w)


def attention_kernel(slots, scal_ref, qa_ref, qb_ref, came_ref, *out_refs):
    column, line, oldest = scal_ref[0], scal_ref[1], scal_ref[2]
    key_block = lax.broadcasted_iota(jnp.int32, (1, COLS * ROWS), 1) // ROWS
    key_rank = (key_block * LINE + line - oldest) & (BLOCKS - 1)
    ranks, places = [], []
    for slot in slots:
        places.append((line + AWAY[slot]) & (LINE - 1))
        ranks.append((column * LINE + places[-1] - oldest) & (BLOCKS - 1))
    upper = lax.broadcasted_iota(jnp.int32, (2 * ROWS, 1), 0) < ROWS
    seen = key_rank <= jnp.where(upper, ranks[0], ranks[1])
    lane = lax.broadcasted_iota(jnp.int32, (ROWS, 128), 1)
    totals = []
    for h in range(NH):
        at = slice(h * ROWS, (h + 1) * ROWS)
        q = jnp.concatenate([qa_ref[at, :], qb_ref[at, :]], axis=0)
        keys = came_ref[:, at, :].reshape(COLS * ROWS, HD)
        values = came_ref[:, QROWS + h * ROWS : QROWS + (h + 1) * ROWS, :].reshape(
            COLS * ROWS, HD
        )
        weights = jnp.where(seen, jnp.exp(dot_t(q, keys)), 0.0)
        totals.append(jnp.sum(weights, axis=-1, keepdims=True))
        products = dot(weights.astype(BF16), values)
        for b in range(2):
            out_refs[b][at, :] = products[b * ROWS : (b + 1) * ROWS].astype(out_refs[b].dtype)
    root = oldest // LINE
    mine = line == (oldest & (LINE - 1))
    for b in range(2):
        tile = jnp.zeros((ROWS, 128), F32)
        for h in range(NH):
            total = totals[h][b * ROWS : (b + 1) * ROWS]
            tile = jnp.where(lane == h, total, tile)
        out_refs[b][QROWS:BACK, :] = parted(tile.T[0:8]).astype(out_refs[b].dtype)
        at = pl.multiple_of(KV + places[b] * 16, 16)
        extra = jnp.concatenate(
            [came_ref[root, pl.ds(at, 16), :], came_ref[root, KV + 128 : SEND, :]], axis=0
        ).astype(F32)
        out_refs[b][BACK:RETURN, :] = jnp.where(mine, extra, 0.0).astype(out_refs[b].dtype)


def parted(totals):
    high = totals.astype(BF16).astype(F32)
    return jnp.concatenate([high, totals - high], axis=0)


def partial_attention(scal, slots, queries, came, kind):
    shape = jax.ShapeDtypeStruct((RETURN, HD), kind)
    return pl.pallas_call(
        functools.partial(attention_kernel, slots),
        out_shape=(shape, shape),
        in_specs=[smem()] + vmem(3),
        out_specs=tuple(vmem(2)),
        compiler_params=params(16),
        name="attention",
    )(scal, *[queries[slot] for slot in slots], came)


def joined_kernel(*refs):
    count = len(refs) // 3
    for i in range(count):
        came_ref, own_ref, out_ref = refs[i], refs[count + i], refs[2 * count + i]
        sums = came_ref[...].astype(F32) + own_ref[...]
        out_ref[0:QROWS, :] = sums[0:QROWS].astype(BF16)
        out_ref[QROWS:BACK, :] = parted(sums[QROWS : QROWS + 8] + sums[QROWS + 8 : BACK]).astype(
            BF16
        )
        out_ref[BACK:RETURN, :] = sums[BACK:RETURN].astype(BF16)


def joined(came, own):
    shape = jax.ShapeDtypeStruct((RETURN, HD), BF16)
    return pl.pallas_call(
        joined_kernel,
        out_shape=(shape,) * len(came),
        in_specs=vmem(2 * len(came)),
        out_specs=tuple(vmem(len(came))),
        compiler_params=params(16),
        name="joined",
    )(*came, *own)


def combine_kernel(up_ref, down_ref, own_ref, out_ref, leaving_ref):
    sums = up_ref[...].astype(F32) + down_ref[...].astype(F32) + own_ref[...]
    leaving = sums[BACK:RETURN]
    leaving_ref[...] = leaving
    totals = sums[QROWS : QROWS + 8] + sums[QROWS + 8 : BACK]
    tile = jnp.concatenate([totals, jnp.zeros((ROWS - 8, 128), F32)], axis=0).T
    for h in range(NH):
        total = tile[:, h : h + 1]
        out_ref[0:ROWS, h * HD : (h + 1) * HD] = (sums[h * ROWS : (h + 1) * ROWS] / total).astype(
            BF16
        )
        out_ref[ROWS:OUTROWS, h * HD : (h + 1) * HD] = jnp.concatenate(
            [leaving[2 * h : 2 * h + 2], jnp.zeros((14, HD), F32)], axis=0
        ).astype(BF16)


def combine(up, down, own):
    return pl.pallas_call(
        combine_kernel,
        out_shape=(
            jax.ShapeDtypeStruct((OUTROWS, QROWS), BF16),
            jax.ShapeDtypeStruct((32, HD), F32),
        ),
        in_specs=vmem(3),
        out_specs=tuple(vmem(2)),
        compiler_params=params(16),
        name="combine",
    )(up, down, own)


def finish_kernel(
    scal_ref, att_ref, w1_ref, w2_ref, w3_ref, own_ref, mod_ref, leaving_ref, fresh_ref, w_ref,
    window_ref, clean_ref, w_held, sem,
):
    tensor = scal_ref[3]
    first = pl.multiple_of(tensor * QW, 128)
    copy = pltpu.make_async_copy(w_ref.at[:, pl.ds(first, QW)], w_held, sem)
    copy.start()
    projected = dot(att_ref[tensor ^ 1], w1_ref[...])
    projected = projected + dot(att_ref[tensor ^ 2], w2_ref[...])
    projected = projected + dot(att_ref[tensor ^ 3], w3_ref[...])
    copy.wait()
    projected = projected + dot(att_ref[tensor], w_held[...])
    oldest = scal_ref[0] * LINE + scal_ref[1] == scal_ref[2]
    leaving = leaving_ref[...]
    for k in range(5):
        at = slice(k * 128, (k + 1) * 128)
        states = own_ref[:, at].astype(F32)
        updated = (states + mod_ref[2:3, at] * projected[0:ROWS, at]).astype(BF16)
        window_ref[:, at] = jnp.where(oldest, fresh_ref[:, at], updated)
        gate = leaving[16 + k : 17 + k] + leaving[21 + k : 22 + k]
        old = leaving[2 * (NH + k) : 2 * (NH + k) + 2]
        clean_ref[:, at] = (old + gate * projected[ROWS : ROWS + 2, at]).astype(BF16)


def finish(scal, attended, pieces, own, mod, leaving, fresh, w):
    return pl.pallas_call(
        finish_kernel,
        out_shape=(
            jax.ShapeDtypeStruct((ROWS, QW), BF16),
            jax.ShapeDtypeStruct((2, QW), BF16),
        ),
        in_specs=[smem()] + vmem(8) + [hbm()],
        out_specs=tuple(vmem(2)),
        scratch_shapes=[pltpu.VMEM((QROWS, QW), BF16), pltpu.SemaphoreType.DMA],
        compiler_params=params(16),
        name="finish",
    )(scal, attended, *pieces, own, mod, leaving, fresh, w)


COLUMN, TENSOR = ("yh", "x"), ("yl", "core")


def shifted(array, step):
    return lax.ppermute(array, "z", [(i, (i + step) % LINE) for i in range(LINE)])


def ring(own):
    pieces, up, down = [own], own, own
    for step in range(LINE // 2):
        up = shifted(up, 1)
        pieces.append(up)
        if step < LINE // 2 - 1:
            down = shifted(down, -1)
            pieces.append(down)
    return pieces


def exchanged(weight, after):
    place = lax.axis_index(TENSOR)
    weight, _ = lax.optimization_barrier((weight, after))
    return [
        lax.ppermute(
            lax.dynamic_slice_in_dim(weight, (place ^ d) * QW, QW, 1),
            TENSOR,
            [(i, i ^ d) for i in range(4)],
        )
        for d in (1, 2, 3)
    ]


def local(
    latents, levels, head_slot, fresh_noise, ada_weight, qkv_weight, q_gain, k_gain, out_weight
):
    oldest = head_slot[0]
    scal = jnp.stack(
        [lax.axis_index(COLUMN), lax.axis_index("z"), oldest, lax.axis_index(TENSOR)]
    ).astype(jnp.int32)
    ada = jnp.transpose(ada_weight, (1, 0, 2))
    w = jnp.transpose(qkv_weight, (1, 0, 2))
    mod, normed, own = opening(levels, scal, ada, latents, q_gain[None], k_gain[None])
    mods = lax.all_gather(mod, TENSOR, axis=0, tiled=False)
    q, sent = front(normed, mods, mod, own, w)
    came = lax.all_to_all(sent, COLUMN, 0, 0)
    queries = ring(q)
    came, *queries = lax.optimization_barrier((came, *queries))
    up, down = partial_attention(scal, TURNS[0], queries, came, BF16)
    weights = exchanged(out_weight, down)
    for turn in (1, 2):
        up, down = shifted(up, 1), shifted(down, -1)
        up, down = joined(
            (up, down), partial_attention(scal, TURNS[turn], queries, came, F32)
        )
    up, down = shifted(up, 1), shifted(down, -1)
    still, last = partial_attention(scal, TURNS[3], queries, came, F32)
    still, weights = lax.optimization_barrier((still, weights))
    down = shifted(joined((down,), (last,))[0], -1)
    attended, leaving = combine(up, down, still)
    attended = lax.all_gather(attended, TENSOR, axis=0, tiled=False)
    return finish(scal, attended, weights, own, mod, leaving, fresh_noise, out_weight)


def solution(mesh):
    fine = Mesh(mesh.devices.reshape(2, 4, 8, 2, 2), ("yh", "x", "z", "yl", "core"))
    seq, tensor = ("yh", "x", "z"), ("yl", "core")
    return jax.shard_map(
        local,
        mesh=fine,
        in_specs=(
            P(seq, None),
            P(seq),
            P(),
            P(None, tensor),
            P(None, None, tensor),
            P(None, None, tensor),
            P(),
            P(),
            P(tensor, None),
        ),
        out_specs=(P(seq, tensor), P(seq, tensor)),
        check_vma=False,
    )
```

```python
import functools
import math

import jax
import jax.numpy as jnp
from jax import lax
from jax.experimental import pallas as pl
from jax.experimental.pallas import tpu as pltpu
from jax.sharding import Mesh
from jax.sharding import PartitionSpec as P

F32 = jnp.float32
BF16 = jnp.bfloat16
COLS = 8
LINE = 8
BLOCKS = COLS * LINE
ROWS = 128
HD = 128
NH = 3
D = 2560
QW = D // 4
QROWS = NH * ROWS
KV = 2 * QROWS
EXTRA = 144
SEND = KV + EXTRA
BACK = QROWS + 16
RETURN = BACK + 32
OUTROWS = ROWS + 16
AWAY = (0, -1, 1, -2, 2, -3, 3, 4)
TURNS = ((6, 7), (4, 5), (2, 3), (0, 1))


LONG = pl.CostEstimate(flops=10_000_000_000, transcendentals=0, bytes_accessed=20_000_000)


def vmem(n):
    return [pl.BlockSpec(memory_space=pltpu.VMEM)] * n


def hbm():
    return pl.BlockSpec(memory_space=pltpu.MemorySpace.HBM)


def smem():
    return pl.BlockSpec(memory_space=pltpu.SMEM)


def params(mib=48):
    return pltpu.CompilerParams(vmem_limit_bytes=mib << 20)


def dot(a, b):
    return jnp.dot(a, b, preferred_element_type=F32)


def dot_t(a, b):
    return lax.dot_general(a, b, (((1,), (1,)), ((), ())), preferred_element_type=F32)


def embedding_kernel(level_ref, out_ref):
    half = 128
    index = lax.broadcasted_iota(jnp.int32, (16, 2 * half), 1)
    place = jnp.where(index < half, index, index - half).astype(F32)
    frequency = jnp.exp(-math.log(10000.0) * place / half)
    angle = level_ref[0].astype(F32) * frequency
    wave = jnp.where(index < half, jnp.cos(angle), jnp.sin(angle))
    out_ref[...] = (wave * (1.0 / (1.0 + jnp.exp(-wave)))).astype(BF16)


def embedded(levels):
    return pl.pallas_call(
        embedding_kernel,
        out_shape=jax.ShapeDtypeStruct((16, 256), BF16),
        in_specs=[smem()],
        out_specs=vmem(1)[0],
        compiler_params=params(16),
        cost_estimate=LONG,
        name="embedding",
    )(levels)


def opening_kernel(
    emb_ref, scal_ref, ada_ref, lat_ref, qg_ref, kg_ref, mod_ref, normed_ref, own_ref
):
    for j in range(3):
        mod_ref[pl.ds(j, 1), :] = dot(emb_ref[...], ada_ref[j])[0:1]
    mod_ref[3:4, 0:HD] = qg_ref[...]
    mod_ref[4:5, 0:HD] = kg_ref[...]
    states = lat_ref[...].astype(F32)
    average = jnp.mean(states, axis=-1, keepdims=True)
    centered = states - average
    variance = jnp.mean(centered * centered, axis=-1, keepdims=True)
    normed_ref[...] = centered * lax.rsqrt(variance + 1e-06)
    first = pl.multiple_of(scal_ref[2] * QW, 128)
    for k in range(5):
        own_ref[:, k * 128 : (k + 1) * 128] = lat_ref[:, pl.ds(first + k * 128, 128)]


def opening(embedding, scal, ada, latents, q_gain, k_gain):
    return pl.pallas_call(
        opening_kernel,
        out_shape=(
            jax.ShapeDtypeStruct((8, QW), F32),
            jax.ShapeDtypeStruct((ROWS, D), F32),
            jax.ShapeDtypeStruct((ROWS, QW), BF16),
        ),
        in_specs=vmem(1) + [smem()] + vmem(4),
        out_specs=tuple(vmem(3)),
        compiler_params=params(16),
        cost_estimate=LONG,
        name="opening",
    )(embedding, scal, ada, latents, q_gain, k_gain)


def rms_rounded(matrix, gain, factor):
    power = jnp.mean(matrix * matrix, axis=-1, keepdims=True)
    return (matrix * lax.rsqrt(power + 1e-06) * gain * factor).astype(BF16)


def front_kernel(
    normed_ref, mods_ref, mod_ref, own_ref, w_ref, q_ref, out_ref, hidden_ref, piece_ref, cut_ref
):
    for t in range(4):
        piece = normed_ref[:, t * QW : (t + 1) * QW]
        shift = mods_ref[t, 0:1, :]
        scale = mods_ref[t, 1:2, :]
        hidden_ref[:, t * QW : (t + 1) * QW] = (piece * (1.0 + scale) + shift).astype(BF16)
    for k in range(5):
        piece_ref[NH + k] = own_ref[:, k * 128 : (k + 1) * 128].astype(F32)
    rows = [mod_ref[2:3, k * 128 : (k + 1) * 128] for k in range(5)]
    high = [row.astype(BF16).astype(F32) for row in rows]
    low = [row - top for row, top in zip(rows, high)]
    gate = jnp.concatenate(high + low + [jnp.zeros((6, 128), F32)], axis=0).astype(BF16)
    hidden = hidden_ref[...]
    keys_all = dot(hidden, w_ref[1])
    values_all = dot(hidden, w_ref[2])
    queries_all = dot(hidden, w_ref[0])
    for h in range(NH):
        at = slice(h * HD, (h + 1) * HD)
        keys = rms_rounded(keys_all[:, at], mod_ref[4:5, 0:HD], 1.0)
        values = values_all[:, at].astype(BF16)
        q = rms_rounded(queries_all[:, at], mod_ref[3:4, 0:HD], 1.0 / math.sqrt(HD))
        q_ref[at, :] = q
        for c in range(COLS):
            out_ref[c, h * ROWS : (h + 1) * ROWS, :] = keys
            out_ref[c, QROWS + h * ROWS : QROWS + (h + 1) * ROWS, :] = values
        weights = jnp.exp(dot_t(q, keys))
        total = jnp.sum(weights, axis=-1, keepdims=True)
        attended = (dot(weights.astype(BF16), values) / total).astype(BF16)
        piece_ref[h] = attended.astype(F32)
    for k in range(8):
        for r in range(2):
            cut_ref[pl.ds(2 * k + r, BLOCKS, stride=16), :] = piece_ref[
                k, pl.ds(r, BLOCKS, stride=2), :
            ]
    for c in range(COLS):
        out_ref[c, KV : KV + 128, :] = cut_ref[c * 128 : (c + 1) * 128, :].astype(BF16)
        out_ref[c, KV + 128 : SEND, :] = gate


def front(normed, mods, mod, own, w):
    return pl.pallas_call(
        front_kernel,
        out_shape=(
            jax.ShapeDtypeStruct((QROWS, HD), BF16),
            jax.ShapeDtypeStruct((COLS, SEND, HD), BF16),
        ),
        in_specs=vmem(5),
        out_specs=tuple(vmem(2)),
        scratch_shapes=[
            pltpu.VMEM((ROWS, D), BF16),
            pltpu.VMEM((8, ROWS, 128), F32),
            pltpu.VMEM((BLOCKS * 16, 128), F32),
        ],
        compiler_params=params(16),
        name="front",
    )(normed, mods, mod, own, w)


def attention_kernel(slots, scal_ref, slot_ref, qa_ref, qb_ref, came_ref, *out_refs):
    column, line, oldest = scal_ref[0], scal_ref[1], slot_ref[0]
    key_block = lax.broadcasted_iota(jnp.int32, (1, COLS * ROWS), 1) // ROWS
    key_rank = (key_block * LINE + line - oldest) & (BLOCKS - 1)
    ranks, places = [], []
    for slot in slots:
        places.append((line + AWAY[slot]) & (LINE - 1))
        ranks.append((column * LINE + places[-1] - oldest) & (BLOCKS - 1))
    upper = lax.broadcasted_iota(jnp.int32, (2 * ROWS, 1), 0) < ROWS
    seen = key_rank <= jnp.where(upper, ranks[0], ranks[1])
    lane = lax.broadcasted_iota(jnp.int32, (ROWS, 128), 1)
    totals = []
    for h in range(NH):
        at = slice(h * ROWS, (h + 1) * ROWS)
        q = jnp.concatenate([qa_ref[at, :], qb_ref[at, :]], axis=0)
        keys = came_ref[:, at, :].reshape(COLS * ROWS, HD)
        values = came_ref[:, QROWS + h * ROWS : QROWS + (h + 1) * ROWS, :].reshape(
            COLS * ROWS, HD
        )
        weights = jnp.where(seen, jnp.exp(dot_t(q, keys)), 0.0)
        totals.append(jnp.sum(weights, axis=-1, keepdims=True))
        products = dot(weights.astype(BF16), values)
        for b in range(2):
            out_refs[b][at, :] = products[b * ROWS : (b + 1) * ROWS].astype(out_refs[b].dtype)
    root = oldest // LINE
    mine = line == (oldest & (LINE - 1))
    for b in range(2):
        tile = jnp.zeros((ROWS, 128), F32)
        for h in range(NH):
            total = totals[h][b * ROWS : (b + 1) * ROWS]
            tile = jnp.where(lane == h, total, tile)
        out_refs[b][QROWS:BACK, :] = parted(tile.T[0:8]).astype(out_refs[b].dtype)
        at = pl.multiple_of(KV + places[b] * 16, 16)
        extra = jnp.concatenate(
            [came_ref[root, pl.ds(at, 16), :], came_ref[root, KV + 128 : SEND, :]], axis=0
        ).astype(F32)
        out_refs[b][BACK:RETURN, :] = jnp.where(mine, extra, 0.0).astype(out_refs[b].dtype)


def parted(totals):
    high = totals.astype(BF16).astype(F32)
    return jnp.concatenate([high, totals - high], axis=0)


def partial_attention(scal, head_slot, slots, queries, came, kind):
    shape = jax.ShapeDtypeStruct((RETURN, HD), kind)
    return pl.pallas_call(
        functools.partial(attention_kernel, slots),
        out_shape=(shape, shape),
        in_specs=[smem(), smem()] + vmem(3),
        out_specs=tuple(vmem(2)),
        compiler_params=params(16),
        name="attention",
    )(scal, head_slot, *[queries[slot] for slot in slots], came)


def joined_kernel(*refs):
    count = len(refs) // 3
    for i in range(count):
        came_ref, own_ref, out_ref = refs[i], refs[count + i], refs[2 * count + i]
        sums = came_ref[...].astype(F32) + own_ref[...]
        out_ref[0:QROWS, :] = sums[0:QROWS].astype(BF16)
        out_ref[QROWS:BACK, :] = parted(sums[QROWS : QROWS + 8] + sums[QROWS + 8 : BACK]).astype(
            BF16
        )
        out_ref[BACK:RETURN, :] = sums[BACK:RETURN].astype(BF16)


def joined(came, own):
    shape = jax.ShapeDtypeStruct((RETURN, HD), BF16)
    return pl.pallas_call(
        joined_kernel,
        out_shape=(shape,) * len(came),
        in_specs=vmem(2 * len(came)),
        out_specs=tuple(vmem(len(came))),
        compiler_params=params(16),
        name="joined",
    )(*came, *own)


def combine_kernel(up_ref, down_ref, own_ref, out_ref, leaving_ref):
    sums = up_ref[...].astype(F32) + down_ref[...].astype(F32) + own_ref[...]
    leaving = sums[BACK:RETURN]
    leaving_ref[...] = leaving
    totals = sums[QROWS : QROWS + 8] + sums[QROWS + 8 : BACK]
    tile = jnp.concatenate([totals, jnp.zeros((ROWS - 8, 128), F32)], axis=0).T
    for h in range(NH):
        total = tile[:, h : h + 1]
        out_ref[0:ROWS, h * HD : (h + 1) * HD] = (sums[h * ROWS : (h + 1) * ROWS] / total).astype(
            BF16
        )
        out_ref[ROWS:OUTROWS, h * HD : (h + 1) * HD] = jnp.concatenate(
            [leaving[2 * h : 2 * h + 2], jnp.zeros((14, HD), F32)], axis=0
        ).astype(BF16)


def combine(up, down, own):
    return pl.pallas_call(
        combine_kernel,
        out_shape=(
            jax.ShapeDtypeStruct((OUTROWS, QROWS), BF16),
            jax.ShapeDtypeStruct((32, HD), F32),
        ),
        in_specs=vmem(3),
        out_specs=tuple(vmem(2)),
        compiler_params=params(16),
        cost_estimate=LONG,
        name="combine",
    )(up, down, own)


def finish_kernel(
    scal_ref, slot_ref, att_ref, w1_ref, w2_ref, w3_ref, own_ref, mod_ref, leaving_ref, fresh_ref, w_ref,
    window_ref, clean_ref, w_held, sem,
):
    tensor = scal_ref[2]
    first = pl.multiple_of(tensor * QW, 128)
    copy = pltpu.make_async_copy(w_ref.at[:, pl.ds(first, QW)], w_held, sem)
    copy.start()
    projected = dot(att_ref[tensor ^ 1], w1_ref[...])
    projected = projected + dot(att_ref[tensor ^ 2], w2_ref[...])
    projected = projected + dot(att_ref[tensor ^ 3], w3_ref[...])
    copy.wait()
    projected = projected + dot(att_ref[tensor], w_held[...])
    oldest = scal_ref[0] * LINE + scal_ref[1] == slot_ref[0]
    leaving = leaving_ref[...]
    for k in range(5):
        at = slice(k * 128, (k + 1) * 128)
        states = own_ref[:, at].astype(F32)
        updated = (states + mod_ref[2:3, at] * projected[0:ROWS, at]).astype(BF16)
        window_ref[:, at] = jnp.where(oldest, fresh_ref[:, at], updated)
        gate = leaving[16 + k : 17 + k] + leaving[21 + k : 22 + k]
        old = leaving[2 * (NH + k) : 2 * (NH + k) + 2]
        clean_ref[:, at] = (old + gate * projected[ROWS : ROWS + 2, at]).astype(BF16)


def finish(scal, head_slot, attended, pieces, own, mod, leaving, fresh, w):
    return pl.pallas_call(
        finish_kernel,
        out_shape=(
            jax.ShapeDtypeStruct((ROWS, QW), BF16),
            jax.ShapeDtypeStruct((2, QW), BF16),
        ),
        in_specs=[smem(), smem()] + vmem(8) + [hbm()],
        out_specs=tuple(vmem(2)),
        scratch_shapes=[pltpu.VMEM((QROWS, QW), BF16), pltpu.SemaphoreType.DMA],
        compiler_params=params(16),
        name="finish",
    )(scal, head_slot, attended, *pieces, own, mod, leaving, fresh, w)


COLUMN, TENSOR = ("yh", "x"), ("yl", "core")


def shifted(array, step):
    return lax.ppermute(array, "z", [(i, (i + step) % LINE) for i in range(LINE)])


def ring(own):
    pieces, up, down = [own], own, own
    for step in range(LINE // 2):
        up = shifted(up, 1)
        pieces.append(up)
        if step < LINE // 2 - 1:
            down = shifted(down, -1)
            pieces.append(down)
    return pieces


def exchanged(weight, after):
    place = lax.axis_index(TENSOR)
    weight, _ = lax.optimization_barrier((weight, after))
    return [
        lax.ppermute(
            lax.dynamic_slice_in_dim(weight, (place ^ d) * QW, QW, 1),
            TENSOR,
            [(i, i ^ d) for i in range(4)],
        )
        for d in (1, 2, 3)
    ]


def local(
    latents, levels, head_slot, fresh_noise, ada_weight, qkv_weight, q_gain, k_gain, out_weight
):
    scal = jnp.stack(
        [lax.axis_index(COLUMN), lax.axis_index("z"), lax.axis_index(TENSOR)]
    ).astype(jnp.int32)
    ada = jnp.transpose(ada_weight, (1, 0, 2))
    w = jnp.transpose(qkv_weight, (1, 0, 2))
    mod, normed, own = opening(
        embedded(levels), scal, ada, latents, q_gain[None], k_gain[None]
    )
    mods = lax.all_gather(mod, TENSOR, axis=0, tiled=False)
    q, sent = front(normed, mods, mod, own, w)
    came = lax.all_to_all(sent, COLUMN, 0, 0)
    queries = ring(q)
    came, *queries = lax.optimization_barrier((came, *queries))
    up, down = partial_attention(scal, head_slot, TURNS[0], queries, came, BF16)
    weights = exchanged(out_weight, down)
    for turn in (1, 2):
        up, down = shifted(up, 1), shifted(down, -1)
        parts = partial_attention(scal, head_slot, TURNS[turn], queries, came, F32)
        up, down = joined((up, down), parts)
    up, down = shifted(up, 1), shifted(down, -1)
    still, last = partial_attention(scal, head_slot, TURNS[3], queries, came, F32)
    still, weights = lax.optimization_barrier((still, weights))
    down = shifted(joined((down,), (last,))[0], -1)
    attended, leaving = combine(up, down, still)
    attended = lax.all_gather(attended, TENSOR, axis=0, tiled=False)
    return finish(scal, head_slot, attended, weights, own, mod, leaving, fresh_noise, out_weight)


def solution(mesh):
    fine = Mesh(mesh.devices.reshape(2, 4, 8, 2, 2), ("yh", "x", "z", "yl", "core"))
    seq, tensor = ("yh", "x", "z"), ("yl", "core")
    return jax.shard_map(
        local,
        mesh=fine,
        in_specs=(
            P(seq, None),
            P(seq),
            P(),
            P(None, tensor),
            P(None, None, tensor),
            P(None, None, tensor),
            P(),
            P(),
            P(tensor, None),
        ),
        out_specs=(P(seq, tensor), P(seq, tensor)),
        check_vma=False,
    )
```

```python
import functools
import math

import jax
import jax.numpy as jnp
from jax import lax
from jax.experimental import pallas as pl
from jax.experimental.pallas import tpu as pltpu
from jax.sharding import Mesh
from jax.sharding import PartitionSpec as P

F32 = jnp.float32
BF16 = jnp.bfloat16
COLS = 8
LINE = 8
BLOCKS = COLS * LINE
ROWS = 128
HD = 128
NH = 3
D = 2560
QW = D // 4
QROWS = NH * ROWS
KV = 2 * QROWS
EXTRA = 144
SEND = KV + EXTRA
BACK = QROWS + 16
RETURN = BACK + 32
OUTROWS = ROWS + 16
AWAY = (0, -1, 1, -2, 2, -3, 3, 4)
TURNS = ((6, 7), (4, 5), (2, 3), (0, 1))


LONG = pl.CostEstimate(flops=10_000_000_000, transcendentals=0, bytes_accessed=20_000_000)


def vmem(n):
    return [pl.BlockSpec(memory_space=pltpu.VMEM)] * n


def hbm():
    return pl.BlockSpec(memory_space=pltpu.MemorySpace.HBM)


def smem():
    return pl.BlockSpec(memory_space=pltpu.SMEM)


def params(mib=48):
    return pltpu.CompilerParams(vmem_limit_bytes=mib << 20)


def dot(a, b):
    return jnp.dot(a, b, preferred_element_type=F32)


def dot_t(a, b):
    return lax.dot_general(a, b, (((1,), (1,)), ((), ())), preferred_element_type=F32)


def embedding_kernel(level_ref, out_ref):
    half = 128
    index = lax.broadcasted_iota(jnp.int32, (16, 2 * half), 1)
    place = jnp.where(index < half, index, index - half).astype(F32)
    frequency = jnp.exp(-math.log(10000.0) * place / half)
    angle = level_ref[0].astype(F32) * frequency
    wave = jnp.where(index < half, jnp.cos(angle), jnp.sin(angle))
    out_ref[...] = (wave * (1.0 / (1.0 + jnp.exp(-wave)))).astype(BF16)


def embedded(levels):
    return pl.pallas_call(
        embedding_kernel,
        out_shape=jax.ShapeDtypeStruct((16, 256), BF16),
        in_specs=[smem()],
        out_specs=vmem(1)[0],
        compiler_params=params(16),
        cost_estimate=LONG,
        name="embedding",
    )(levels)


def opening_kernel(
    emb_ref, scal_ref, ada_ref, lat_ref, qg_ref, kg_ref, mod_ref, normed_ref, own_ref
):
    for j in range(3):
        mod_ref[pl.ds(j, 1), :] = dot(emb_ref[...], ada_ref[j])[0:1]
    mod_ref[3:4, 0:HD] = qg_ref[...]
    mod_ref[4:5, 0:HD] = kg_ref[...]
    states = lat_ref[...].astype(F32)
    average = jnp.mean(states, axis=-1, keepdims=True)
    centered = states - average
    variance = jnp.mean(centered * centered, axis=-1, keepdims=True)
    normed_ref[...] = centered * lax.rsqrt(variance + 1e-06)
    first = pl.multiple_of(scal_ref[2] * QW, 128)
    for k in range(5):
        own_ref[:, k * 128 : (k + 1) * 128] = lat_ref[:, pl.ds(first + k * 128, 128)]


def opening(embedding, scal, ada, latents, q_gain, k_gain):
    return pl.pallas_call(
        opening_kernel,
        out_shape=(
            jax.ShapeDtypeStruct((8, QW), F32),
            jax.ShapeDtypeStruct((ROWS, D), F32),
            jax.ShapeDtypeStruct((ROWS, QW), BF16),
        ),
        in_specs=vmem(1) + [smem()] + vmem(4),
        out_specs=tuple(vmem(3)),
        compiler_params=params(16),
        cost_estimate=LONG,
        name="opening",
    )(embedding, scal, ada, latents, q_gain, k_gain)


def rms_rounded(matrix, gain, factor):
    power = jnp.mean(matrix * matrix, axis=-1, keepdims=True)
    return (matrix * lax.rsqrt(power + 1e-06) * gain * factor).astype(BF16)


def front_kernel(
    normed_ref, mods_ref, mod_ref, own_ref, w_ref, q_ref, out_ref, hidden_ref, piece_ref, cut_ref
):
    for t in range(4):
        piece = normed_ref[:, t * QW : (t + 1) * QW]
        shift = mods_ref[t, 0:1, :]
        scale = mods_ref[t, 1:2, :]
        hidden_ref[:, t * QW : (t + 1) * QW] = (piece * (1.0 + scale) + shift).astype(BF16)
    for k in range(5):
        piece_ref[NH + k] = own_ref[:, k * 128 : (k + 1) * 128].astype(F32)
    rows = [mod_ref[2:3, k * 128 : (k + 1) * 128] for k in range(5)]
    high = [row.astype(BF16).astype(F32) for row in rows]
    low = [row - top for row, top in zip(rows, high)]
    gate = jnp.concatenate(high + low + [jnp.zeros((6, 128), F32)], axis=0).astype(BF16)
    hidden = hidden_ref[...]
    keys_all = dot(hidden, w_ref[1])
    values_all = dot(hidden, w_ref[2])
    queries_all = dot(hidden, w_ref[0])
    for h in range(NH):
        at = slice(h * HD, (h + 1) * HD)
        keys = rms_rounded(keys_all[:, at], mod_ref[4:5, 0:HD], 1.0)
        values = values_all[:, at].astype(BF16)
        q = rms_rounded(queries_all[:, at], mod_ref[3:4, 0:HD], 1.0 / math.sqrt(HD))
        q_ref[at, :] = q
        for c in range(COLS):
            out_ref[c, h * ROWS : (h + 1) * ROWS, :] = keys
            out_ref[c, QROWS + h * ROWS : QROWS + (h + 1) * ROWS, :] = values
        weights = jnp.exp(dot_t(q, keys))
        total = jnp.sum(weights, axis=-1, keepdims=True)
        attended = (dot(weights.astype(BF16), values) / total).astype(BF16)
        piece_ref[h] = attended.astype(F32)
    for k in range(8):
        for r in range(2):
            cut_ref[pl.ds(2 * k + r, BLOCKS, stride=16), :] = piece_ref[
                k, pl.ds(r, BLOCKS, stride=2), :
            ]
    for c in range(COLS):
        out_ref[c, KV : KV + 128, :] = cut_ref[c * 128 : (c + 1) * 128, :].astype(BF16)
        out_ref[c, KV + 128 : SEND, :] = gate


def front(normed, mods, mod, own, w):
    return pl.pallas_call(
        front_kernel,
        out_shape=(
            jax.ShapeDtypeStruct((QROWS, HD), BF16),
            jax.ShapeDtypeStruct((COLS, SEND, HD), BF16),
        ),
        in_specs=vmem(5),
        out_specs=tuple(vmem(2)),
        scratch_shapes=[
            pltpu.VMEM((ROWS, D), BF16),
            pltpu.VMEM((8, ROWS, 128), F32),
            pltpu.VMEM((BLOCKS * 16, 128), F32),
        ],
        compiler_params=params(16),
        name="front",
    )(normed, mods, mod, own, w)


def attention_kernel(slots, scal_ref, slot_ref, qa_ref, qb_ref, came_ref, *out_refs):
    column, line, oldest = scal_ref[0], scal_ref[1], slot_ref[0]
    key_block = lax.broadcasted_iota(jnp.int32, (1, COLS * ROWS), 1) // ROWS
    key_rank = (key_block * LINE + line - oldest) & (BLOCKS - 1)
    ranks, places = [], []
    for slot in slots:
        places.append((line + AWAY[slot]) & (LINE - 1))
        ranks.append((column * LINE + places[-1] - oldest) & (BLOCKS - 1))
    upper = lax.broadcasted_iota(jnp.int32, (2 * ROWS, 1), 0) < ROWS
    seen = key_rank <= jnp.where(upper, ranks[0], ranks[1])
    lane = lax.broadcasted_iota(jnp.int32, (ROWS, 128), 1)
    totals = []
    for h in range(NH):
        at = slice(h * ROWS, (h + 1) * ROWS)
        q = jnp.concatenate([qa_ref[at, :], qb_ref[at, :]], axis=0)
        keys = came_ref[:, at, :].reshape(COLS * ROWS, HD)
        values = came_ref[:, QROWS + h * ROWS : QROWS + (h + 1) * ROWS, :].reshape(
            COLS * ROWS, HD
        )
        weights = jnp.where(seen, jnp.exp(dot_t(q, keys)), 0.0)
        totals.append(jnp.sum(weights, axis=-1, keepdims=True))
        products = dot(weights.astype(BF16), values)
        for b in range(2):
            out_refs[b][at, :] = products[b * ROWS : (b + 1) * ROWS].astype(out_refs[b].dtype)
    root = oldest // LINE
    mine = line == (oldest & (LINE - 1))
    for b in range(2):
        tile = jnp.zeros((ROWS, 128), F32)
        for h in range(NH):
            total = totals[h][b * ROWS : (b + 1) * ROWS]
            tile = jnp.where(lane == h, total, tile)
        out_refs[b][QROWS:BACK, :] = parted(tile.T[0:8]).astype(out_refs[b].dtype)
        at = pl.multiple_of(KV + places[b] * 16, 16)
        extra = jnp.concatenate(
            [came_ref[root, pl.ds(at, 16), :], came_ref[root, KV + 128 : SEND, :]], axis=0
        ).astype(F32)
        out_refs[b][BACK:RETURN, :] = jnp.where(mine, extra, 0.0).astype(out_refs[b].dtype)


def parted(totals):
    high = totals.astype(BF16).astype(F32)
    return jnp.concatenate([high, totals - high], axis=0)


def partial_attention(scal, head_slot, slots, queries, came, kind):
    shape = jax.ShapeDtypeStruct((RETURN, HD), kind)
    return pl.pallas_call(
        functools.partial(attention_kernel, slots),
        out_shape=(shape, shape),
        in_specs=[smem(), smem()] + vmem(3),
        out_specs=tuple(vmem(2)),
        compiler_params=params(16),
        name="attention",
    )(scal, head_slot, *[queries[slot] for slot in slots], came)


def joined_kernel(*refs):
    count = len(refs) // 3
    for i in range(count):
        came_ref, own_ref, out_ref = refs[i], refs[count + i], refs[2 * count + i]
        sums = came_ref[...].astype(F32) + own_ref[...]
        out_ref[0:QROWS, :] = sums[0:QROWS].astype(BF16)
        out_ref[QROWS:BACK, :] = parted(sums[QROWS : QROWS + 8] + sums[QROWS + 8 : BACK]).astype(
            BF16
        )
        out_ref[BACK:RETURN, :] = sums[BACK:RETURN].astype(BF16)


def joined(came, own):
    shape = jax.ShapeDtypeStruct((RETURN, HD), BF16)
    return pl.pallas_call(
        joined_kernel,
        out_shape=(shape,) * len(came),
        in_specs=vmem(2 * len(came)),
        out_specs=tuple(vmem(len(came))),
        compiler_params=params(16),
        name="joined",
    )(*came, *own)


def combine_kernel(up_ref, down_ref, own_ref, out_ref, leaving_ref):
    sums = up_ref[...].astype(F32) + down_ref[...].astype(F32) + own_ref[...]
    leaving = sums[BACK:RETURN]
    leaving_ref[...] = leaving
    totals = sums[QROWS : QROWS + 8] + sums[QROWS + 8 : BACK]
    tile = jnp.concatenate([totals, jnp.zeros((ROWS - 8, 128), F32)], axis=0).T
    for h in range(NH):
        total = tile[:, h : h + 1]
        out_ref[0:ROWS, h * HD : (h + 1) * HD] = (sums[h * ROWS : (h + 1) * ROWS] / total).astype(
            BF16
        )
        out_ref[ROWS:OUTROWS, h * HD : (h + 1) * HD] = jnp.concatenate(
            [leaving[2 * h : 2 * h + 2], jnp.zeros((14, HD), F32)], axis=0
        ).astype(BF16)


def combine(up, down, own):
    return pl.pallas_call(
        combine_kernel,
        out_shape=(
            jax.ShapeDtypeStruct((OUTROWS, QROWS), BF16),
            jax.ShapeDtypeStruct((32, HD), F32),
        ),
        in_specs=vmem(3),
        out_specs=tuple(vmem(2)),
        compiler_params=params(16),
        cost_estimate=LONG,
        name="combine",
    )(up, down, own)


def finish_kernel(
    scal_ref, slot_ref, att_ref, w0_ref, w1_ref, w2_ref, w3_ref, own_ref, mod_ref, leaving_ref,
    fresh_ref, window_ref, clean_ref,
):
    tensor = scal_ref[2]
    projected = dot(att_ref[tensor], w0_ref[...])
    for d, w_ref in enumerate((w1_ref, w2_ref, w3_ref), 1):
        projected = projected + dot(att_ref[tensor ^ d], w_ref[...])
    oldest = scal_ref[0] * LINE + scal_ref[1] == slot_ref[0]
    leaving = leaving_ref[...]
    for k in range(5):
        at = slice(k * 128, (k + 1) * 128)
        states = own_ref[:, at].astype(F32)
        updated = (states + mod_ref[2:3, at] * projected[0:ROWS, at]).astype(BF16)
        window_ref[:, at] = jnp.where(oldest, fresh_ref[:, at], updated)
        gate = leaving[16 + k : 17 + k] + leaving[21 + k : 22 + k]
        old = leaving[2 * (NH + k) : 2 * (NH + k) + 2]
        clean_ref[:, at] = (old + gate * projected[ROWS : ROWS + 2, at]).astype(BF16)


def finish(scal, head_slot, attended, pieces, own, mod, leaving, fresh):
    return pl.pallas_call(
        finish_kernel,
        out_shape=(
            jax.ShapeDtypeStruct((ROWS, QW), BF16),
            jax.ShapeDtypeStruct((2, QW), BF16),
        ),
        in_specs=[smem(), smem()] + vmem(9),
        out_specs=tuple(vmem(2)),
        compiler_params=params(16),
        name="finish",
    )(scal, head_slot, attended, *pieces, own, mod, leaving, fresh)


COLUMN, TENSOR = ("yh", "x"), ("yl", "core")


def shifted(array, step):
    return lax.ppermute(array, "z", [(i, (i + step) % LINE) for i in range(LINE)])


def ring(own):
    pieces, up, down = [own], own, own
    for step in range(LINE // 2):
        up = shifted(up, 1)
        pieces.append(up)
        if step < LINE // 2 - 1:
            down = shifted(down, -1)
            pieces.append(down)
    return pieces


def exchanged(weight, after):
    place = lax.axis_index(TENSOR)
    weight, _ = lax.optimization_barrier((weight, after))
    parts = [
        lax.dynamic_slice_in_dim(weight, (place ^ d) * QW, QW, 1) for d in range(4)
    ]
    return parts[:1] + [
        lax.ppermute(parts[d], TENSOR, [(i, i ^ d) for i in range(4)]) for d in (1, 2, 3)
    ]


def local(
    latents, levels, head_slot, fresh_noise, ada_weight, qkv_weight, q_gain, k_gain, out_weight
):
    scal = jnp.stack(
        [lax.axis_index(COLUMN), lax.axis_index("z"), lax.axis_index(TENSOR)]
    ).astype(jnp.int32)
    ada = jnp.transpose(ada_weight, (1, 0, 2))
    w = jnp.transpose(qkv_weight, (1, 0, 2))
    mod, normed, own = opening(
        embedded(levels), scal, ada, latents, q_gain[None], k_gain[None]
    )
    mods = lax.all_gather(mod, TENSOR, axis=0, tiled=False)
    q, sent = front(normed, mods, mod, own, w)
    came = lax.all_to_all(sent, COLUMN, 0, 0)
    queries = ring(q)
    came, *queries = lax.optimization_barrier((came, *queries))
    up, down = partial_attention(scal, head_slot, TURNS[0], queries, came, BF16)
    weights = exchanged(out_weight, down)
    for turn in (1, 2):
        up, down = shifted(up, 1), shifted(down, -1)
        parts = partial_attention(scal, head_slot, TURNS[turn], queries, came, F32)
        up, down = joined((up, down), parts)
    up, down = shifted(up, 1), shifted(down, -1)
    still, last = partial_attention(scal, head_slot, TURNS[3], queries, came, F32)
    still, weights = lax.optimization_barrier((still, weights))
    down = shifted(joined((down,), (last,))[0], -1)
    attended, leaving = combine(up, down, still)
    attended = lax.all_gather(attended, TENSOR, axis=0, tiled=False)
    return finish(scal, head_slot, attended, weights, own, mod, leaving, fresh_noise)


def solution(mesh):
    fine = Mesh(mesh.devices.reshape(2, 4, 8, 2, 2), ("yh", "x", "z", "yl", "core"))
    seq, tensor = ("yh", "x", "z"), ("yl", "core")
    return jax.shard_map(
        local,
        mesh=fine,
        in_specs=(
            P(seq, None),
            P(seq),
            P(),
            P(None, tensor),
            P(None, None, tensor),
            P(None, None, tensor),
            P(),
            P(),
            P(tensor, None),
        ),
        out_specs=(P(seq, tensor), P(seq, tensor)),
        check_vma=False,
    )
```
